256 devices in a mesh: dp: 16 (over z, x_lo), ctx: 16 (over x_hi, y, core).
Axes of the slice: x: 4 (x_hi: 2, x_lo: 2; x = x_hi * 2 + x_lo), y: 4, z: 8, core: 2. Of those that a mesh axis runs over, the one named last changes fastest.
Arguments:
- normed: bfloat16 [16, 4096, 2048], P('dp', 'ctx'), may hold values from -21 to 21
- token_ids: int32 [16, 4096], P('dp', 'ctx'), may hold values from 0 to 128255
- block_order: int32 [16], replicated, may hold values from 0 to 15, each once
- master_weight: float32 [2048, 3072], P(('dp', 'ctx')), may hold values from -0.125 to 0.125
- weight_grad: float32 [2048, 3072], P(('dp', 'ctx')), may hold values from -6 to 6
- moment_one: float32 [2048, 3072], P(('dp', 'ctx')), may hold values from -4 to 4
- moment_two: float32 [2048, 3072], P(('dp', 'ctx')), may hold values from 0.1 to 3
Outputs:
- new_master: float32 [2048, 3072], P(('dp', 'ctx'))
- new_moment_one: float32 [2048, 3072], P(('dp', 'ctx'))
- new_moment_two: float32 [2048, 3072], P(('dp', 'ctx'))
- attended: bfloat16 [16, 4096, 2048], P('dp', 'ctx')
The draws below stay inside these ranges and needn't reach their ends.
All inputs are finite; a program needn't handle non-finite values.
Results may differ from the reference program's by a relative error of at most 0.008.
The reference program's roundings to bfloat16 on the way count: a program that leaves them out, or rounds other values in their place, can miss the bound.
Values may be sent and summed in bfloat16 or wider, within the bound.
A program may use at most 64 MiB of HBM per device.

```python
import math
import jax
import jax.numpy as jnp
from jax import lax

D = 2048
HQ = 16
HK = 4
DH = 128
VOCAB = 128256
TOK_DEV = 256
QKV = 3072
GROUP = 4
BATCH = 16
SEQ = 4096
DOC_GAP = 2048
N_CTX = 16


def draw_normed(key, part):
    base_key = jax.random.fold_in(key, 0)
    values = jnp.clip(jax.random.normal(base_key, (BATCH, SEQ, D), jnp.float32), -6.0, 6.0)
    return values.astype(jnp.bfloat16)


def set_ends(result, stream_key, least, largest):
    index_at = [jax.random.randint(jax.random.fold_in(stream_key, axis), (), 0, length) for axis, length in enumerate(result.shape)]
    widest = result.shape.index(max(result.shape))
    next_to = index_at[:widest] + [(index_at[widest] + 1) % result.shape[widest]] + index_at[widest + 1:]
    return result.at[tuple(index_at)].set(least).at[tuple(next_to)].set(largest)


def block_scale(own_key, shape, cuts, least, top_value):
    factor_of = 1.0
    for axis_at, shards_of in cuts:
        heights = jax.random.uniform(jax.random.fold_in(jax.random.fold_in(own_key, 6), axis_at), (shards_of,), jnp.float32, least / len(cuts), top_value / len(cuts))
        factor_of = factor_of * jnp.repeat(jnp.exp(heights), shape[axis_at] // shards_of).reshape((-1,) + (1,) * (len(shape) - 1 - axis_at))
    return factor_of


def centred(own_key, extent, deviation, bound, pieces=(), held_as=jnp.bfloat16):
    values = jax.random.normal(own_key, extent, jnp.float32) * deviation
    if len(pieces) > 0:
        values = block_scale(own_key, extent, pieces, -0.22, 0.18) * values
    return jnp.clip(values, min=-bound, max=bound).astype(held_as)


def setup_inputs(seed: int = 0) -> dict:
    splits = jax.random.split(jax.random.key(seed), 8)
    return {
        "normed": draw_normed(jax.random.fold_in(splits[7], 71), 0),
        "token_ids": set_ends(jax.random.randint(splits[1], (BATCH, SEQ), 0, VOCAB), jax.random.fold_in(splits[1], 1), 0, VOCAB - 1).astype(jnp.int32),
        "block_order": jax.random.permutation(splits[2], N_CTX).astype(jnp.int32),
        "master_weight": centred(splits[3], (D, QKV), D ** -0.5, 0.125, ((0, 256),), jnp.float32),
        "weight_grad": centred(splits[4], (D, QKV), 1.0, 6.0, ((0, 256),), jnp.float32),
        "moment_one": centred(splits[5], (D, QKV), 0.3, 4.0, ((0, 256),), jnp.float32),
        "moment_two": jnp.clip(jnp.exp(math.log(3.0) - 3.4011974 * jax.random.uniform(splits[6], (D, QKV), jnp.float32) ** block_scale(splits[6], (D, QKV), ((0, 256),), -0.2, 0.2)), 0.1, 3.0),
    }


beta_one = 0.9
beta_two = 0.95
adam_step = 10.0
learn_rate = 0.0003
decay_rate = 0.1
adam_eps = 1e-08
rope_theta = 500000.0
masked_score = -1e+30

def adam_update(master_weight, weight_grad, moment_one, moment_two):
    fresh_one = beta_one * moment_one + (1.0 - beta_one) * weight_grad
    fresh_two = beta_two * moment_two + (1.0 - beta_two) * weight_grad * weight_grad
    fix_one = 1.0 - beta_one ** adam_step
    fix_two = 1.0 - beta_two ** adam_step
    step_size = fresh_one / fix_one / (jnp.sqrt(fresh_two / fix_two) + adam_eps)
    fresh_master = master_weight - learn_rate * (step_size + decay_rate * master_weight)
    return (fresh_master, fresh_one, fresh_two)

def rotate(values, positions):
    half_dim = values.shape[-1] // 2
    frequency = rope_theta ** (-2.0 * jnp.arange(half_dim, dtype=jnp.float32) / values.shape[-1])
    angles = positions.astype(jnp.float32)[:, None] * frequency[None, :]
    cosine = jnp.cos(angles)[:, None, :]
    sine_part = jnp.sin(angles)[:, None, :]
    first_half = values[..., :half_dim]
    second_half = values[..., half_dim:]
    return jnp.concatenate([first_half * cosine - second_half * sine_part, second_half * cosine + first_half * sine_part], -1)

def reference(normed, token_ids, block_order, master_weight, weight_grad, moment_one, moment_two):
    new_master, new_moment_one, new_moment_two = adam_update(master_weight, weight_grad, moment_one, moment_two)
    fresh_weight = new_master.astype(jnp.bfloat16)
    score_scale = DH ** (-0.5)
    row_index = jnp.arange(SEQ, dtype=jnp.int32)
    positions = (block_order[row_index // TOK_DEV] * TOK_DEV + row_index % TOK_DEV).astype(jnp.int32)

    def one_sequence(pair):
        normed_row, id_row = pair
        marks = jnp.where(id_row % DOC_GAP == 0, positions, 0).astype(jnp.int32)
        in_order = jnp.zeros((SEQ,), jnp.int32).at[positions].set(marks)
        doc_start = lax.cummax(in_order, axis=0)[positions]
        projected = jnp.dot(normed_row, fresh_weight, preferred_element_type=jnp.float32)
        queries = rotate(projected[:, :HQ * DH].reshape(SEQ, HQ, DH), positions).astype(jnp.bfloat16)
        key_rows = rotate(projected[:, HQ * DH:(HQ + HK) * DH].reshape(SEQ, HK, DH), positions).astype(jnp.bfloat16)
        value_rows = projected[:, (HQ + HK) * DH:].reshape(SEQ, HK, DH).astype(jnp.bfloat16)
        queries = lax.optimization_barrier(queries).astype(jnp.float32)
        key_rows = lax.optimization_barrier(key_rows).astype(jnp.float32)
        value_rows = lax.optimization_barrier(value_rows).astype(jnp.float32)

        def query_block(block_index):
            first_row = (block_index * TOK_DEV).astype(jnp.int32)
            block_q = lax.dynamic_slice_in_dim(queries, first_row, TOK_DEV, 0).reshape(TOK_DEV, HK, GROUP, DH)
            q_pos = lax.dynamic_slice_in_dim(positions, first_row, TOK_DEV, 0)
            q_start = lax.dynamic_slice_in_dim(doc_start, first_row, TOK_DEV, 0)
            scores = jnp.einsum('qgjd,kgd->gjqk', block_q, key_rows) * score_scale
            allowed = (positions[None, :] <= q_pos[:, None]) & (positions[None, :] >= q_start[:, None])
            scores = jnp.where(allowed, scores, masked_score)
            row_max = lax.optimization_barrier(jnp.max(scores, -1, keepdims=True))
            weights = jnp.where(allowed, jnp.exp(scores - row_max), 0.0)
            denominators = lax.optimization_barrier(jnp.sum(weights, -1))
            rounded = lax.optimization_barrier(weights.astype(jnp.bfloat16)).astype(jnp.float32)
            mixed_out = jnp.einsum('gjqk,kgd->qgjd', rounded, value_rows)
            mixed_out = mixed_out / jnp.transpose(denominators, (2, 0, 1))[..., None]
            return mixed_out.reshape(TOK_DEV, HQ * DH).astype(jnp.bfloat16)
        blocks = lax.map(query_block, jnp.arange(N_CTX, dtype=jnp.int32))
        return blocks.reshape(SEQ, HQ * DH)
    attended = lax.map(one_sequence, (normed, token_ids))
    return (new_master, new_moment_one, new_moment_two, attended)
```

```python
import functools
import math

import jax
import jax.numpy as jnp
from jax import lax
from jax.experimental import pallas as pl
from jax.experimental.pallas import tpu as pltpu
from jax.sharding import PartitionSpec as P

HQ = 16
HK = 4
DH = 128
GROUP = 4
BLK = 256
D = 2048

beta_one = 0.9
beta_two = 0.95
adam_step = 10.0
learn_rate = 0.0003
decay_rate = 0.1
adam_eps = 1e-08
rope_theta = 500000.0
masked_score = -1e30
MESH = pl.DeviceIdType.MESH
LOG_SCALE = DH**-0.5 * math.log2(math.e)


def adam_update(master_weight, weight_grad, moment_one, moment_two):
    fresh_one = beta_one * moment_one + (1.0 - beta_one) * weight_grad
    fresh_two = beta_two * moment_two + (1.0 - beta_two) * weight_grad * weight_grad
    fix_one = 1.0 - beta_one**adam_step
    fix_two = 1.0 - beta_two**adam_step
    step_size = fresh_one / fix_one / (jnp.sqrt(fresh_two / fix_two) + adam_eps)
    fresh_master = master_weight - learn_rate * (step_size + decay_rate * master_weight)
    return (fresh_master, fresh_one, fresh_two)


class Place:
    def __init__(self):
        dp = lax.axis_index("dp")
        ctx = lax.axis_index("ctx")
        self.z, x_lo = dp // 2, dp % 2
        x_hi = ctx // 8
        self.y = (ctx // 2) % 4
        self.core = ctx % 2
        self.x = x_hi * 2 + x_lo

    def at(self, x=None, y=None, z=None, core=None):
        x = self.x if x is None else x
        y = self.y if y is None else y
        z = self.z if z is None else z
        core = self.core if core is None else core
        return (z * 2 + x % 2, (x // 2) * 8 + y * 2 + core)


class Sender:
    def __init__(self, send_sem, recv_sem):
        self.send_sem, self.recv_sem, self.started = send_sem, recv_sem, []

    def __call__(self, src, dst, device):
        n = len(self.started)
        copy = pltpu.make_async_remote_copy(
            src_ref=src,
            dst_ref=dst,
            send_sem=self.send_sem.at[n],
            recv_sem=self.recv_sem.at[n],
            device_id=device,
            device_id_type=MESH,
        )
        copy.start()
        self.started.append(copy)
        return copy

    def drain(self):
        for copy in self.started:
            copy.wait_send()


def greet(devices):
    barrier = pltpu.get_barrier_semaphore()
    for device in devices:
        pl.semaphore_signal(barrier, inc=1, device_id=device, device_id_type=MESH)
    pl.semaphore_wait(barrier, len(devices))


def ring(send, n, p, block, half, device):
    right, left = device((p + 1) % n), device((p + n - 1) % n)
    to_right = send(block(p), block(p), right)
    to_left = send(block(p), block(p), left)
    yield
    for step in range(1, n // 2):
        from_left, from_right = (p + n - step) % n, (p + step) % n
        piece = block if step < n // 2 - 1 else None
        to_right.wait_recv()
        src = piece(from_left) if piece else half(from_left, 0)
        to_right = send(src, src, right)
        to_left.wait_recv()
        src = piece(from_right) if piece else half(from_right, 1)
        to_left = send(src, src, left)
        yield
    to_right.wait_recv()
    to_left.wait_recv()


def gather_kernel(
    x_ref, w_ref, lm_ref, mark_ref, before_ref, cos_ref, sin_ref,
    q_ref, kv_ref, ds_ref,
    wbuf, x2, lm2, mk, send_sem, recv_sem, own_sem,
):
    me = Place()
    x, y, z, core = me.x, me.y, me.z, me.core
    xs = (x % 2) * 2 + x // 2
    other = 1 - core
    partner = me.at(core=other)

    def slot(xv):
        return (xv % 2) * 2 + xv // 2

    rows = pl.ds(pl.multiple_of(core * 8, 8), 8)
    own = [
        pltpu.make_async_copy(w_ref.at[core], wbuf.at[:, z, xs, y, rows, :], own_sem.at[0]),
        pltpu.make_async_copy(x_ref, x2.at[core], own_sem.at[1]),
        pltpu.make_async_copy(lm_ref, lm2.at[core], own_sem.at[2]),
        pltpu.make_async_copy(mark_ref, mk.at[xs, y, core], own_sem.at[3]),
    ]
    for copy in own:
        copy.start()
    greet(
        [partner]
        + [me.at(x=(x + d) % 4) for d in (1, 3)]
        + [me.at(y=(y + d) % 4) for d in (1, 3)]
        + [me.at(z=(z + d) % 8) for d in (1, 7)]
    )
    send = Sender(send_sem, recv_sem)
    w_there = send(w_ref.at[other], wbuf.at[:, z, xs, y, rows, :], partner)
    mark_there = send(mark_ref, mk.at[xs, y, core], partner)
    x_there = send(x_ref, x2.at[core], partner)
    lm_there = send(lm_ref, lm2.at[core], partner)
    own[0].wait()
    own[3].wait()
    w_there.wait_recv()
    mark_there.wait_recv()

    def by_x(xv):
        return me.at(x=xv)

    def by_y(yv):
        return me.at(y=yv)

    def by_z(zv):
        return me.at(z=zv)

    cols = (pl.ds(0, 256), pl.ds(256, 256))

    def color_zero():
        w = wbuf.at[0]
        yield from ring(send, 4, x, lambda v: w.at[z, slot(v), y], lambda v, h: w.at[z, slot(v), y, :, cols[h]], by_x)
        yield from ring(send, 4, y, lambda v: w.at[z, :, v], lambda v, h: w.at[z, pl.ds(2 * h, 2), v], by_y)
        yield from ring(send, 8, z, lambda v: w.at[v], lambda v, h: w.at[v, pl.ds(2 * h, 2)], by_z)

    def color_one():
        w = wbuf.at[1]
        yield from ring(send, 4, y, lambda v: w.at[z, xs, v], lambda v, h: w.at[z, xs, v, :, cols[h]], by_y)
        yield from ring(send, 8, z, lambda v: w.at[v, xs], lambda v, h: w.at[v, xs, pl.ds(2 * h, 2)], by_z)
        yield from ring(send, 4, x, lambda v: w.at[:, slot(v)], lambda v, h: w.at[pl.ds(4 * h, 4), slot(v)], by_x)

    def color_two():
        w = wbuf.at[2]
        yield from ring(send, 8, z, lambda v: w.at[v, xs, y], lambda v, h: w.at[v, xs, y, :, cols[h]], by_z)
        yield from ring(send, 4, x, lambda v: w.at[:, slot(v), y], lambda v, h: w.at[pl.ds(4 * h, 4), slot(v), y], by_x)
        yield from ring(send, 4, y, lambda v: w.at[:, :, v], lambda v, h: w.at[pl.ds(4 * h, 4), :, v], by_y)

    def marks():
        yield from ring(send, 4, y, lambda v: mk.at[xs, v], lambda v, h: mk.at[xs, v, pl.ds(h, 1)], by_y)
        yield from ring(send, 4, x, lambda v: mk.at[slot(v)], lambda v, h: mk.at[slot(v), pl.ds(2 * h, 2)], by_x)

    chains = [color_zero(), color_one(), color_two(), marks()]

    def project(color):
        rows_in = x2[...].reshape(2 * BLK, D)
        return jnp.dot(rows_in, wbuf[color].reshape(D, 512), preferred_element_type=jnp.float32)

    def rotated(part):
        turned = pltpu.roll(part, DH // 2, 1)
        return (part * cos_ref[...] + turned * sin_ref[...]).astype(jnp.bfloat16)

    def queries(color):
        out = project(color)
        for h in range(4):
            q_ref[color * 4 + h] = rotated(out[:, h * DH : (h + 1) * DH])

    order = [0, 1, 2, 3] * 4 + [0, 1, 2, 3] + [1, 2, 1, 2, 0, 0, 1, 2, 0]
    for chain in order:
        next(chains[chain], None)
    own[1].wait()
    own[2].wait()
    x_there.wait_recv()
    lm_there.wait_recv()
    x_lo = x % 2
    heard = mk[pl.ds(x_lo * 2, 2)].reshape(16, 8, 128)
    for b in range(2):
        prior = jnp.max(heard * before_ref[b], axis=0)
        ds_ref[b * BLK : (b + 1) * BLK, :] = jnp.maximum(lm2[b], prior[0:1, :])
    for _ in chains[0]:
        pass
    queries(0)
    for _ in chains[1]:
        pass
    queries(1)
    for _ in chains[2]:
        pass
    for _ in chains[3]:
        pass
    out = project(2)
    for g in range(2):
        kv_ref[g, :, :DH] = rotated(out[:, g * 256 : g * 256 + DH])
        kv_ref[g, :, DH:] = out[:, g * 256 + DH : (g + 1) * 256].astype(jnp.bfloat16)
    send.drain()


def attend_kernel(
    q_ref, kv_ref, ds_ref, qpos_ref, kpos_ref,
    out_ref,
    kvbuf, relay_a, relay_b, m_ref, l_ref, acc_ref, bias_ref, ostage,
    send_sem, recv_sem, own_sem,
):
    me = Place()
    x, y, core = me.x, me.y, me.core
    xh = x // 2
    far = 1 - xh
    other = 1 - core
    partner = me.at(core=other)
    own = pltpu.make_async_copy(kv_ref, kvbuf.at[:, xh, y], own_sem)
    own.start()
    right_x, left_x = me.at(x=(x + 1) % 4), me.at(x=(x + 3) % 4)
    right_y, left_y = me.at(y=(y + 1) % 4), me.at(y=(y + 3) % 4)
    greet([partner, right_x, left_x, right_y, left_y])
    send = Sender(send_sem, recv_sem)
    lo, hi = pl.ds(0, BLK), pl.ds(BLK, BLK)
    y_r, y_l, y_f = (y + 1) % 4, (y + 3) % 4, (y + 2) % 4
    from_left_x, from_right_x = ((x + 3) % 4) // 2, ((x + 1) % 4) // 2

    def first_leg(src, relay):
        return send(src.at[lo], relay(0), right_x), send(src.at[hi], relay(1), left_x)

    def second_leg(legs, relay, head, yv):
        legs[0].wait_recv()
        one = send(relay(0), kvbuf.at[head, from_left_x, yv, lo], right_x)
        legs[1].wait_recv()
        two = send(relay(1), kvbuf.at[head, from_right_x, yv, hi], left_x)
        return one, two

    def landed(pair):
        for copy in pair:
            copy.wait_recv()

    def rel_a(d):
        return relay_a.at[d]

    def rel_b(k):
        return lambda d: relay_b.at[d, k]

    def piece(head, xv, yv, first=False):
        chip = xv * 4 + yv
        kpos = kpos_ref[chip][0:1, :]
        for r in range(4):
            part = slice(r * 128, (r + 1) * 128)
            qpos = qpos_ref[part, 0:1]
            start = ds_ref[part, 0:1]
            allowed = (kpos <= qpos) & (kpos >= start)
            bias_ref[part, :] = jnp.where(allowed, 0.0, masked_score)

        def one_head(j, carry):
            h = head * GROUP + j
            keys = kvbuf[head, xv, yv, :, :DH]
            values = kvbuf[head, xv, yv, :, DH:]

            def raw(r):
                return lax.dot_general(
                    q_ref[h, r * 128 : (r + 1) * 128, :], keys, (((1,), (1,)), ((), ())),
                    preferred_element_type=jnp.float32,
                )

            ahead = raw(0)
            for r in range(4):
                part = slice(r * 128, (r + 1) * 128)
                s = ahead * LOG_SCALE + bias_ref[part, :]
                if r < 3:
                    ahead = raw(r + 1)
                top = jnp.broadcast_to(jnp.max(s, axis=1, keepdims=True), (128, 128))
                if not first:
                    old = m_ref[h, part, :]
                    top = jnp.maximum(old, top)
                    fade = jnp.exp2(old - top)
                m_ref[h, part, :] = top
                p = jnp.exp2(s - jnp.tile(top, (1, 4)))
                total = p[:, 0:128] + p[:, 128:256] + p[:, 256:384] + p[:, 384:512]
                pv = jnp.dot(p.astype(jnp.bfloat16), values, preferred_element_type=jnp.float32)
                if first:
                    l_ref[h, part, :] = total
                    acc_ref[h, part, :] = pv
                else:
                    l_ref[h, part, :] = l_ref[h, part, :] * fade + total
                    acc_ref[h, part, :] = acc_ref[h, part, :] * fade + pv
            return carry

        lax.fori_loop(0, GROUP, one_head, 0)

    def finish(head):
        rows_there = pl.ds(pl.multiple_of(other * BLK, BLK), BLK)
        rows_here = pl.ds(pl.multiple_of(core * BLK, BLK), BLK)
        for j in range(GROUP):
            h = head * GROUP + j
            under = jnp.sum(l_ref[h, rows_there, :], axis=1, keepdims=True)
            ostage[head, :, j * DH : (j + 1) * DH] = (acc_ref[h, rows_there, :] / under).astype(jnp.bfloat16)
        for j in range(GROUP):
            h = head * GROUP + j
            under = jnp.sum(l_ref[h, rows_here, :], axis=1, keepdims=True)
            at = pl.ds(pl.multiple_of(core * (8 * DH) + h * DH, DH), DH)
            out_ref[:, at] = (acc_ref[h, rows_here, :] / under).astype(jnp.bfloat16)
        at = pl.ds(pl.multiple_of(core * (8 * DH) + head * GROUP * DH, GROUP * DH), GROUP * DH)
        return send(ostage.at[head], out_ref.at[:, at], partner)

    a_x = first_leg(kv_ref.at[0], rel_a)
    b_y = (send(kv_ref.at[1], kvbuf.at[1, xh, y], right_y), send(kv_ref.at[1], kvbuf.at[1, xh, y], left_y))
    b_x0 = first_leg(kv_ref.at[1], rel_b(0))
    own.wait()
    piece(1, xh, y, True)
    a_far = second_leg(a_x, rel_a, 0, y)
    piece(0, xh, y, True)
    landed(b_y)
    b_f = (
        send(kvbuf.at[1, xh, y_l, lo], kvbuf.at[1, xh, y_l, lo], right_y),
        send(kvbuf.at[1, xh, y_r, hi], kvbuf.at[1, xh, y_r, hi], left_y),
    )
    b_x1 = first_leg(kvbuf.at[1, xh, y_l], rel_b(1))
    b_x2 = first_leg(kvbuf.at[1, xh, y_r], rel_b(2))
    piece(1, xh, y_l)
    landed(a_far)
    a_y = (
        send(kvbuf.at[0, :, y], kvbuf.at[0, :, y], right_y),
        send(kvbuf.at[0, :, y], kvbuf.at[0, :, y], left_y),
    )
    b_far0 = second_leg(b_x0, rel_b(0), 1, y)
    piece(1, xh, y_r)
    landed(b_f)
    b_x3 = first_leg(kvbuf.at[1, xh, y_f], rel_b(3))
    piece(0, far, y)
    b_far1 = second_leg(b_x1, rel_b(1), 1, y_l)
    piece(1, xh, y_f)
    landed(b_far0)
    b_far2 = second_leg(b_x2, rel_b(2), 1, y_r)
    piece(1, far, y)
    landed(a_y)
    a_f = (
        send(kvbuf.at[0, :, y_l, lo], kvbuf.at[0, :, y_l, lo], right_y),
        send(kvbuf.at[0, :, y_r, hi], kvbuf.at[0, :, y_r, hi], left_y),
    )
    b_far3 = second_leg(b_x3, rel_b(3), 1, y_f)
    piece(0, xh, y_l)
    piece(0, far, y_l)
    piece(0, xh, y_r)
    piece(0, far, y_r)
    landed(b_far1)
    piece(1, far, y_l)
    landed(b_far2)
    piece(1, far, y_r)
    landed(a_f)
    piece(0, xh, y_f)
    piece(0, far, y_f)
    done_a = finish(0)
    landed(b_far3)
    piece(1, far, y_f)
    done_b = finish(1)
    landed((done_a, done_b))
    send.drain()


VMEM = pl.BlockSpec(memory_space=pltpu.VMEM)


def local(normed, token_ids, block_order, master_weight, weight_grad, moment_one, moment_two):
    new_master, new_moment_one, new_moment_two = adam_update(
        master_weight, weight_grad, moment_one, moment_two
    )
    fresh = new_master.astype(jnp.bfloat16)
    halves = []
    for c in range(2):
        k0, v0 = 2048 + 256 * c, 2560 + 256 * c
        joined = jnp.concatenate(
            [fresh[:, k0 : k0 + 128], fresh[:, v0 : v0 + 128], fresh[:, k0 + 128 : k0 + 256], fresh[:, v0 + 128 : v0 + 256]], 1
        )
        halves.append(jnp.stack([fresh[:, 1024 * c : 1024 * c + 512], fresh[:, 1024 * c + 512 : 1024 * c + 1024], joined]))
    w_own = jnp.stack(halves)

    ctx = lax.axis_index("ctx")
    local_idx = jnp.arange(BLK, dtype=jnp.int32)
    my_block = block_order[ctx]
    positions = my_block * BLK + local_idx
    doc_gap = BLK * 16 // 2
    marks = jnp.where(token_ids[0] % doc_gap == 0, positions, 0)
    running = lax.cummax(marks, axis=0)
    lm = jnp.broadcast_to(running[:, None], (BLK, 128))
    mark_tile = jnp.broadcast_to(jnp.max(marks), (8, 128))
    pair = lax.dynamic_slice_in_dim(block_order, ctx - ctx % 2, 2)
    before = jnp.broadcast_to(
        (block_order[None, :] < pair[:, None]).astype(jnp.int32)[:, :, None, None], (2, 16, 8, 128)
    )
    pair_pos = (pair[:, None] * BLK + local_idx[None, :]).reshape(2 * BLK)
    half = DH // 2
    frequency = rope_theta ** (-2.0 * jnp.arange(half, dtype=jnp.float32) / DH)
    angles = pair_pos.astype(jnp.float32)[:, None] * frequency[None, :]
    cosine, sine = jnp.cos(angles), jnp.sin(angles)
    cos_full = jnp.concatenate([cosine, cosine], 1)
    sin_full = jnp.concatenate([-sine, sine], 1)
    qpos = jnp.broadcast_to(pair_pos[:, None], (2 * BLK, 128))
    kpos = (block_order[:, None] * BLK + local_idx[None, :]).reshape(8, 1, 2 * BLK)
    kpos = jnp.broadcast_to(kpos, (8, 8, 2 * BLK))

    q, kv, ds = pl.pallas_call(
        gather_kernel,
        out_shape=(
            jax.ShapeDtypeStruct((8, 2 * BLK, DH), jnp.bfloat16),
            jax.ShapeDtypeStruct((2, 2 * BLK, 2 * DH), jnp.bfloat16),
            jax.ShapeDtypeStruct((2 * BLK, 128), jnp.int32),
        ),
        in_specs=[VMEM] * 7,
        out_specs=[VMEM] * 3,
        scratch_shapes=[
            pltpu.VMEM((3, 8, 4, 4, 16, 512), jnp.bfloat16),
            pltpu.VMEM((2, BLK, D), jnp.bfloat16),
            pltpu.VMEM((2, BLK, 128), jnp.int32),
            pltpu.VMEM((4, 4, 2, 8, 128), jnp.int32),
            pltpu.SemaphoreType.DMA((64,)),
            pltpu.SemaphoreType.DMA((64,)),
            pltpu.SemaphoreType.DMA((4,)),
        ],
        compiler_params=pltpu.CompilerParams(
            collective_id=0, has_side_effects=True, vmem_limit_bytes=40 << 20
        ),
        name="gather_project",
    )(normed[0], w_own, lm, mark_tile, before, cos_full, sin_full)

    attended = pl.pallas_call(
        attend_kernel,
        out_shape=jax.ShapeDtypeStruct((BLK, HQ * DH), jnp.bfloat16),
        in_specs=[VMEM] * 5,
        out_specs=VMEM,
        scratch_shapes=[
            pltpu.VMEM((2, 2, 4, 2 * BLK, 2 * DH), jnp.bfloat16),
            pltpu.VMEM((2, BLK, 2 * DH), jnp.bfloat16),
            pltpu.VMEM((2, 4, BLK, 2 * DH), jnp.bfloat16),
            pltpu.VMEM((8, 2 * BLK, 128), jnp.float32),
            pltpu.VMEM((8, 2 * BLK, 128), jnp.float32),
            pltpu.VMEM((8, 2 * BLK, DH), jnp.float32),
            pltpu.VMEM((2 * BLK, 2 * BLK), jnp.float32),
            pltpu.VMEM((2, BLK, GROUP * DH), jnp.bfloat16),
            pltpu.SemaphoreType.DMA((32,)),
            pltpu.SemaphoreType.DMA((32,)),
            pltpu.SemaphoreType.DMA,
        ],
        compiler_params=pltpu.CompilerParams(
            collective_id=1, has_side_effects=True, vmem_limit_bytes=40 << 20
        ),
        name="attend",
    )(q, kv, ds, qpos, kpos)
    return (new_master, new_moment_one, new_moment_two, attended[None])


def solution(mesh):
    in_specs = (
        P("dp", "ctx", None),
        P("dp", "ctx"),
        P(),
        P(("dp", "ctx"), None),
        P(("dp", "ctx"), None),
        P(("dp", "ctx"), None),
        P(("dp", "ctx"), None),
    )
    out_specs = (
        P(("dp", "ctx"), None),
        P(("dp", "ctx"), None),
        P(("dp", "ctx"), None),
        P("dp", "ctx", None),
    )
    return jax.shard_map(local, mesh=mesh, in_specs=in_specs, out_specs=out_specs, check_vma=False)
```
